32 devices in a mesh: dp: 8 (over y, x, core), seq: 4 (over z).
Axes of the slice: x: 2, y: 2, z: 4, core: 2. Of those that a mesh axis runs over, the one named last changes fastest.
Arguments:
- block_input: bfloat16 [16, 1024, 768], P('dp', 'seq'), may hold values from -6 to 6
- cotangent: bfloat16 [16, 1024, 768], P('dp', 'seq'), may hold values from -6 to 6
- segments: int32 [16, 1024], P('dp'), may hold values from 0 to 3, never falling along the last dimension, each value on 1 to 800 neighbouring positions
- norm_gain: bfloat16 [768], P(('dp', 'seq')), may hold values from 0.5 to 1.5
- w_in: bfloat16 [768, 3352], P(('dp', 'seq')), may hold values from -0.21875 to 0.21875
- conv_weight: bfloat16 [4, 1792], P(None, ('dp', 'seq')), may hold values from -3 to 3
- conv_bias: bfloat16 [1792], P(('dp', 'seq')), may hold values from -0.5 to 0.5
- dt_bias: float32 [24], replicated, may hold values from -6 to -2
- a_log: float32 [24], replicated, may hold values from 0 to 2.77
- d_skip: float32 [24], replicated, may hold values from 0.5 to 1.5
- gate_gain: bfloat16 [1536], P(('dp', 'seq')), may hold values from 0.5 to 1.5
- w_out: bfloat16 [1536, 768], P(('dp', 'seq')), may hold values from -0.15625 to 0.15625
Outputs:
- result: bfloat16 [16, 1024, 768], P('dp', 'seq')
- grad_x: bfloat16 [16, 1024, 768], P('dp', 'seq')
- grad_norm_gain: float32 [768], P(('dp', 'seq'))
- grad_w_in: float32 [768, 3352], P(('dp', 'seq'))
- grad_conv_weight: float32 [4, 1792], P(None, ('dp', 'seq'))
- grad_conv_bias: float32 [1792], P(('dp', 'seq'))
- grad_dt_bias: float32 [24], replicated
- grad_a_log: float32 [24], replicated
- grad_d_skip: float32 [24], replicated
- grad_gate_gain: float32 [1536], P(('dp', 'seq'))
- grad_w_out: float32 [1536, 768], P(('dp', 'seq'))
The draws below stay inside these ranges and needn't reach their ends.
Inputs may be any that keep to these rules, and one draw needn't show every extreme that they name: `segments`: along each sequence the numbers start at 0, never fall and rise by one where a new document begins; every document has 1 to 800 tokens, and one document of each sequence has exactly 800.
All inputs are finite; a program needn't handle non-finite values.
Results may differ from the reference program's by a relative error of at most 0.012.
Values may be sent and summed in bfloat16 or wider, within the bound.
A program may use at most 128 MiB of HBM per device.

```python
import math
import jax
import jax.numpy as jnp
import numpy as np
from jax import lax

D = 768
INNER = 1536
HEAD_DIM = 64
STATE = 128
HEADS = 24
XBC = 1792
PROJ = 3352
BLOCK = 256
DOC_MOST = 800
LENGTH = 1024
SEQS = 16
SEGS = 4


def block_scale(key, shape, cuts, low, largest):
    level = 1.0
    for axis_at, shards_of in cuts:
        steps = jax.random.uniform(jax.random.fold_in(jax.random.fold_in(key, 6), axis_at), (shards_of,), jnp.float32, low / len(cuts), largest / len(cuts))
        level = level * jnp.repeat(jnp.exp(steps), shape[axis_at] // shards_of).reshape((-1,) + (1,) * (len(shape) - 1 - axis_at))
    return level


def profile(amount, total, bound, slope):
    loads = [(1 << 20) // math.isqrt(rank ** slope) + 1 for rank in range(2, amount + 1)]
    rest, given = total - bound - (amount - 1), [1] * (amount - 1)
    while rest > 0:
        free = [i for i in range(amount - 1) if given[i] < bound]
        mass, remaining = sum([loads[i] for i in free]), rest
        for i in free:
            extra = min(bound - given[i], max(1, remaining * loads[i] // mass), rest)
            given[i] = given[i] + extra
            rest = rest - extra
    return np.array([bound] + given)


def uneven_parts(rng, amount, total, bound, lean):
    if amount == 2:
        one = jax.random.randint(rng, (), max(1, total - bound), min(bound, total - 1) + 1)
        return jnp.stack([one, total - one])
    lengths = jnp.asarray(profile(amount, total, bound, lean), jnp.int32)
    twos = (amount - 1) // 2
    donor, sink = lengths[1:1 + 2 * twos:2], lengths[2:2 + 2 * twos:2]
    margin = jnp.minimum(donor - 1, bound - sink)
    shifted = jax.random.randint(jax.random.fold_in(rng, 1), (twos,), 0, 1 << 20) % (margin + 1)
    lengths = lengths.at[1:1 + 2 * twos:2].set(donor - shifted).at[2:2 + 2 * twos:2].set(sink + shifted)
    return lengths[jax.random.permutation(jax.random.fold_in(rng, 2), amount)]


def gaussian(rng, dims, spread, most, cuts=(), kind=jnp.bfloat16):
    array = jax.random.normal(rng, dims, jnp.float32) * spread
    if len(cuts) > 0:
        array = block_scale(rng, dims, cuts, -0.22, 0.18) * array
    return jnp.clip(array, min=-most, max=most).astype(kind)


def setup_inputs(seed: int = 0) -> dict:
    splits = jax.random.split(jax.random.key(seed), 13)
    return {
        "block_input": gaussian(splits[0], (SEQS, LENGTH, D), 1.0, 6.0, ((0, 8), (1, 4))),
        "cotangent": gaussian(splits[1], (SEQS, LENGTH, D), 1.0, 6.0, ((0, 8), (1, 4))),
        "segments": jax.vmap(lambda own: jnp.searchsorted(jnp.cumsum(uneven_parts(own, SEGS, LENGTH, DOC_MOST, 0)), jnp.arange(LENGTH), side="right"))(jax.random.split(splits[2], SEQS)).reshape((SEQS, LENGTH)).astype(jnp.int32),
        "norm_gain": jnp.clip(1.0 + 0.1 * jax.random.normal(splits[3], (D,), jnp.float32), 0.5, 1.5).astype(jnp.bfloat16),
        "w_in": gaussian(splits[4], (D, PROJ), D ** -0.5, 0.21875, ((0, 32),)),
        "conv_weight": gaussian(splits[5], (4, XBC), 4 ** -0.5, 3.0, ((1, 32),)),
        "conv_bias": jnp.clip(jax.random.uniform(splits[6], (XBC,), jnp.float32, -0.5, 0.5) * block_scale(splits[6], (XBC,), ((0, 32),), -0.4, 0.0), -0.5, 0.5).astype(jnp.bfloat16),
        "dt_bias": jnp.clip(jax.random.uniform(splits[7], (HEADS,), jnp.float32, -6.0, -2.0), -6.0, -2.0),
        "a_log": jnp.clip(jax.random.uniform(splits[8], (HEADS,), jnp.float32, 0.0, 2.77), 0.0, 2.77),
        "d_skip": jnp.clip(jax.random.uniform(splits[9], (HEADS,), jnp.float32, 0.5, 1.5), 0.5, 1.5),
        "gate_gain": jnp.clip(1.0 + 0.1 * jax.random.normal(splits[10], (INNER,), jnp.float32), 0.5, 1.5).astype(jnp.bfloat16),
        "w_out": gaussian(splits[11], (INNER, D), INNER ** -0.5, 0.15625, ((0, 32),)),
    }


EPSILON = 1e-05
PRECISE = lax.Precision.HIGHEST

@jax.custom_vjp
def low(v):
    return lax.optimization_barrier(v.astype(jnp.bfloat16)).astype(jnp.float32)

@jax.custom_vjp
def low_back(v):
    return v

def low_keep(v):
    return (low(v), None)

def low_pass(kept, grad):
    return (grad,)

def back_keep(v):
    return (v, None)

def back_low(kept, grad):
    return (low(grad),)
low.defvjp(low_keep, low_pass)
low_back.defvjp(back_keep, back_low)

def block_parts(act_block, step_block, cum_block, seg_block, prior_seg):
    x_values = act_block[:, :INNER].reshape(BLOCK, HEADS, HEAD_DIM)
    write_rows = act_block[:, INNER:INNER + STATE]
    read_rows = act_block[:, INNER + STATE:]
    affinity = low_back(jnp.dot(read_rows, write_rows.T, precision=PRECISE))
    positions = jnp.arange(BLOCK)
    same_doc = (seg_block[:, None] == seg_block[None, :]) & (positions[None, :] <= positions[:, None])
    cum_heads = cum_block.T
    exponent = jnp.where(same_doc[None], cum_heads[:, :, None] - cum_heads[:, None, :], -1e+30)
    mixing = low(affinity[None] * jnp.exp(exponent) * step_block.T[:, None, :])
    within = jnp.einsum('hts,shp->thp', mixing, x_values, precision=PRECISE)
    end_same = (seg_block == seg_block[-1]).astype(jnp.float32)
    weight_end = jnp.exp(cum_block[-1] - cum_block) * step_block * end_same[:, None]
    weighted = low(x_values * weight_end[:, :, None])
    local_state = low_back(jnp.einsum('shp,sn->hpn', weighted, write_rows, precision=PRECISE))
    carried = (seg_block == prior_seg).astype(jnp.float32)
    block_decay = jnp.exp(cum_block[-1]) * carried[-1]
    return (within, local_state, block_decay, carried)

def carried_part(read_rows, cum_block, carried, state_in):
    factor = jnp.exp(cum_block) * carried[:, None]
    scaled = low(factor[:, :, None] * read_rows[:, None, :])
    return jnp.einsum('thn,hpn->thp', scaled, low(state_in), precision=PRECISE)

def carry_state(state, pieces):
    local_state, block_decay = pieces
    return (block_decay[:, None, None] * state + local_state, state)

def sequence_forward(tokens, seg_row, weights):
    norm_gain, w_in, conv_weight, conv_bias, dt_bias, a_log, d_skip, gate_gain, w_out = weights
    length = seg_row.shape[0]
    blocks = length // BLOCK
    inv = lax.rsqrt(lax.optimization_barrier(jnp.mean(tokens * tokens, axis=-1, keepdims=True)) + EPSILON)
    normed = low(tokens * inv * norm_gain)
    proj = low_back(low(jnp.dot(normed, w_in, precision=PRECISE)))
    z_rows = proj[:, :INNER]
    xbc_rows = proj[:, INNER:INNER + XBC]
    dt_raw = proj[:, INNER + XBC:]
    xbc_pad = jnp.concatenate([jnp.zeros((3, XBC), jnp.float32), xbc_rows], axis=0)
    seg_pad = jnp.concatenate([jnp.full((3,), -1, jnp.int32), seg_row.astype(jnp.int32)])
    pre = conv_bias
    for offset in range(4):
        valid = (seg_pad[offset:offset + length] == seg_row).astype(jnp.float32)
        pre = pre + conv_weight[offset] * xbc_pad[offset:offset + length] * valid[:, None]
    act = low(jax.nn.silu(pre))
    step_size = jax.nn.softplus(dt_raw + dt_bias)
    log_decay = -jnp.exp(a_log) * step_size
    cum = jnp.cumsum(log_decay.reshape(blocks, BLOCK, HEADS), axis=1)
    seg_blocks = seg_row.reshape(blocks, BLOCK)
    prior = jnp.concatenate([jnp.full((1,), -1, jnp.int32), seg_blocks[:-1, -1].astype(jnp.int32)])
    act_blocks = act.reshape(blocks, BLOCK, XBC)
    within, local_state, block_decay, carried = jax.vmap(block_parts)(act_blocks, step_size.reshape(blocks, BLOCK, HEADS), cum, seg_blocks, prior)
    start_state = jnp.zeros((HEADS, HEAD_DIM, STATE), jnp.float32)
    unused, state_in = lax.scan(carry_state, start_state, (local_state, block_decay))
    from_state = jax.vmap(carried_part)(act_blocks[:, :, INNER + STATE:], cum, carried, state_in)
    x_values = act_blocks[:, :, :INNER].reshape(blocks, BLOCK, HEADS, HEAD_DIM)
    y_values = within + from_state + d_skip[None, None, :, None] * x_values
    y_values = low_back(y_values.reshape(length, INNER))
    gated_in = y_values * jax.nn.silu(z_rows)
    gated = low(gated_in * lax.rsqrt(lax.optimization_barrier(jnp.mean(gated_in * gated_in, axis=-1, keepdims=True)) + EPSILON) * gate_gain)
    return tokens + jnp.dot(gated, w_out, precision=PRECISE)

def reference(block_input, cotangent, segments, norm_gain, w_in, conv_weight, conv_bias, dt_bias, a_log, d_skip, gate_gain, w_out):
    weights = tuple((v.astype(jnp.float32) for v in (norm_gain, w_in, conv_weight, conv_bias, dt_bias, a_log, d_skip, gate_gain, w_out)))
    groups = SEQS // 2
    tokens_all = block_input.astype(jnp.float32).reshape(groups, 2, LENGTH, D)
    cot_all = cotangent.astype(jnp.float32).reshape(groups, 2, LENGTH, D)
    seg_all = segments.astype(jnp.int32).reshape(groups, 2, LENGTH)

    def group_forward(tokens_pair, seg_pair, weight_set):
        return jax.vmap(sequence_forward, in_axes=(0, 0, None))(tokens_pair, seg_pair, weight_set)
    checked = jax.checkpoint(group_forward)

    def forward(tokens_in, weight_set):

        def stepper(carry, inputs):
            return (carry, checked(inputs[0], inputs[1], weight_set))
        unused, outputs = lax.scan(stepper, jnp.zeros((), jnp.float32), (tokens_in, seg_all))
        return outputs
    outputs, pullback = jax.vjp(forward, tokens_all, weights)
    grad_tokens, grad_weights = pullback(cot_all)
    result = outputs.reshape(SEQS, LENGTH, D).astype(jnp.bfloat16)
    grad_input = grad_tokens.reshape(SEQS, LENGTH, D).astype(jnp.bfloat16)
    return (result, grad_input, grad_weights[0], grad_weights[1], grad_weights[2], grad_weights[3], grad_weights[4], grad_weights[5], grad_weights[6], grad_weights[7], grad_weights[8])
```

```python
from functools import partial

import jax
import jax.numpy as jnp
from jax import lax
from jax.sharding import PartitionSpec as P

EPSILON = 1e-05
CONTRACT_ROWS = (((0,), (0,)), ((), ()))
CONTRACT_COLS = (((1,), (1,)), ((), ()))


def hop(value, axis, source, target):
    return lax.ppermute(value, axis, [(source, target)])


def shifted(value, axis, steps):
    count = lax.axis_size(axis)
    initial, last = (max(0, -steps), min(count, count - steps))
    return lax.ppermute(value, axis, [(source, source + steps) for source in range(initial, last)])


def norm_input(tokens_f, gain_f):
    inv = lax.rsqrt(jnp.mean(tokens_f * tokens_f, axis=-1, keepdims=True) + EPSILON)
    return tokens_f * inv * gain_f


def mixer_inputs(xbc_ext, dt_raw, conv_w, conv_b, dt_bias, a_log, tap_mask):
    block_len = dt_raw.shape[1]
    pre = conv_b
    for offset in range(4):
        pre = (
            pre
            + conv_w[offset]
            * xbc_ext[:, offset : offset + block_len]
            * tap_mask[:, :, offset : offset + 1]
        )
    activated = jax.nn.silu(pre)
    step_size = jax.nn.softplus(dt_raw + dt_bias)
    cumulated = jnp.cumsum(-jnp.exp(a_log) * step_size, axis=1)
    return (activated, step_size, cumulated)


def mixing_weights(affinity, cumulated, step_size, same_doc):
    cum_heads = jnp.swapaxes(cumulated, 1, 2)
    exponent = jnp.where(
        same_doc[:, None], cum_heads[:, :, :, None] - cum_heads[:, :, None, :], -1e30
    )
    return affinity[:, None] * jnp.exp(exponent) * jnp.swapaxes(step_size, 1, 2)[:, :, None, :]


def end_weights(cumulated, step_size, end_same, carried_last):
    weight_end = jnp.exp(cumulated[:, -1:] - cumulated) * step_size * end_same[:, :, None]
    block_decay = jnp.exp(cumulated[:, -1]) * carried_last[:, None]
    return (weight_end, block_decay)


def read_scale(read_float, cumulated, carried):
    factor = jnp.exp(cumulated) * carried[:, :, None]
    return factor[:, :, :, None] * read_float[:, :, None, :]


def gate_norm(y_values, z_float, gain_f):
    gated_in = y_values * jax.nn.silu(z_float)
    return (
        gated_in
        * lax.rsqrt(jnp.mean(gated_in * gated_in, axis=-1, keepdims=True) + EPSILON)
        * gain_f
    )


def relay(decay, local, direction):
    count = lax.axis_size("seq")
    chains = []
    for index in range(local.shape[0]):
        incoming = jnp.zeros_like(local[index])
        for step in range(count - 1):
            source = step if direction > 0 else count - 1 - step
            outgoing = decay[index][:, None, None] * incoming + local[index]
            arrived = hop(outgoing.astype(jnp.bfloat16), "seq", source, source + direction)
            incoming = incoming + arrived.astype(jnp.float32)
        chains.append(incoming)
    return jnp.stack(chains)


def per_device(
    block_input,
    cotangent,
    segments,
    norm_gain,
    w_in,
    conv_weight,
    conv_bias,
    dt_bias,
    a_log,
    d_skip,
    gate_gain,
    w_out,
):
    batch, block_len, model_width = block_input.shape
    axes = ("dp", "seq")
    all_devices = lax.axis_size(axes)
    block_start = lax.axis_index("seq") * block_len
    inner_width = gate_gain.shape[0] * all_devices
    head_count = dt_bias.shape[0]
    head_width = inner_width // head_count
    xbc_width = conv_bias.shape[0] * all_devices
    state_width = (xbc_width - inner_width) // 2
    proj_width = w_in.shape[1]
    slab_rows = w_in.shape[0]
    f32 = jnp.float32
    bf16 = jnp.bfloat16

    small_sizes = (norm_gain.size, conv_weight.size, conv_bias.size, gate_gain.size)
    small_cols = -(-sum(small_sizes) // slab_rows)
    smalls = jnp.concatenate(
        [norm_gain, conv_weight.reshape(-1), conv_bias, gate_gain,
         jnp.zeros((small_cols * slab_rows - sum(small_sizes),), bf16)]
    ).reshape(slab_rows, small_cols)
    w_in_full = lax.all_gather(
        jnp.concatenate([w_in, smalls], axis=1), axes, axis=0, tiled=True
    )
    w_out_all = lax.all_gather(w_out, axes, axis=0, tiled=True)
    w_in_all = w_in_full[:, :proj_width]
    small_all = w_in_full[:, proj_width:].reshape(all_devices, slab_rows * small_cols)
    bounds = [0]
    for size in small_sizes:
        bounds.append(bounds[-1] + size)
    gain_all = small_all[:, bounds[0] : bounds[1]].reshape(-1).astype(f32)
    conv_w_all = (
        small_all[:, bounds[1] : bounds[2]]
        .reshape(all_devices, 4, -1)
        .swapaxes(0, 1)
        .reshape(4, xbc_width)
        .astype(f32)
    )
    conv_b_all = small_all[:, bounds[2] : bounds[3]].reshape(-1).astype(f32)
    gate_all = small_all[:, bounds[3] : bounds[4]].reshape(-1).astype(f32)

    tokens_f = block_input.astype(f32)
    normed, norm_back = jax.vjp(norm_input, tokens_f, gain_all)
    normed_b = normed.astype(bf16)
    projected = lax.dot_general(
        normed_b, w_in_all, (((2,), (0,)), ((), ())), preferred_element_type=f32
    ).astype(bf16)
    xbc_rows = projected[:, :, inner_width : inner_width + xbc_width]
    rim_rows = shifted(xbc_rows[:, block_len - 3 :], "seq", 1)
    padded = jnp.concatenate([jnp.full((batch, 3), -1, jnp.int32), segments], axis=1)
    seg_window = lax.dynamic_slice_in_dim(padded, block_start, block_len + 3, axis=1)
    seg_local = seg_window[:, 3:]
    tap_mask = jnp.stack(
        [seg_window[:, offset : offset + block_len] == seg_local for offset in range(4)], axis=2
    ).astype(f32)
    xbc_ext = jnp.concatenate([rim_rows, xbc_rows], axis=1).astype(f32)
    dt_raw = projected[:, :, inner_width + xbc_width :].astype(f32)
    (activated, step_size, cumulated), mixer_back = jax.vjp(
        partial(mixer_inputs, tap_mask=tap_mask),
        xbc_ext,
        dt_raw,
        conv_w_all,
        conv_b_all,
        dt_bias,
        a_log,
    )
    act_b = activated.astype(bf16)
    x_values = act_b[:, :, :inner_width].reshape(batch, block_len, head_count, head_width)
    write_rows = act_b[:, :, inner_width : inner_width + state_width]
    read_rows = act_b[:, :, inner_width + state_width :]
    prior_segment = seg_window[:, 2:3]
    positions = lax.iota(jnp.int32, block_len)
    same_doc = (seg_local[:, :, None] == seg_local[:, None, :]) & (
        positions[None, :] <= positions[:, None]
    )
    carried = (seg_local == prior_segment).astype(f32)
    end_same = (seg_local == seg_local[:, -1:]).astype(f32)
    x_float = x_values.astype(f32)
    read_float = read_rows.astype(f32)
    (weight_end, block_decay), end_back = jax.vjp(
        partial(end_weights, end_same=end_same, carried_last=carried[:, -1]), cumulated, step_size
    )
    weighted_b = (x_float * weight_end[..., None]).astype(bf16)
    local_state = jnp.einsum("bshp,bsn->bhpn", weighted_b, write_rows, preferred_element_type=f32)
    state_in = relay(block_decay, local_state, 1)
    state_b = state_in.astype(bf16)
    affinity = jnp.einsum("btn,bsn->bts", read_rows, write_rows, preferred_element_type=f32)
    mixing, mixing_back = jax.vjp(
        partial(mixing_weights, same_doc=same_doc), affinity, cumulated, step_size
    )
    mixing_b = mixing.astype(bf16)
    within = jnp.einsum("bhts,bshp->bthp", mixing_b, x_values, preferred_element_type=f32)
    scaled, scale_back = jax.vjp(partial(read_scale, carried=carried), read_float, cumulated)
    scaled_b = scaled.astype(bf16)
    from_state = jnp.einsum("bthn,bhpn->bthp", scaled_b, state_b, preferred_element_type=f32)
    y_heads = within + from_state + d_skip[:, None] * x_float
    z_float = projected[:, :, :inner_width].astype(f32)
    gated, gate_back = jax.vjp(
        gate_norm, y_heads.reshape(batch, block_len, inner_width), z_float, gate_all
    )
    gated_b = gated.astype(bf16)
    mixed = lax.dot_general(
        gated_b, w_out_all, (((2,), (0,)), ((), ())), preferred_element_type=f32
    )
    result_rows = (tokens_f + mixed).astype(bf16)
    cot_f = cotangent.astype(f32)
    grad_wout = lax.dot_general(
        gated_b, cotangent, (((0, 1), (0, 1)), ((), ())), preferred_element_type=f32
    ).astype(bf16)
    grad_wout = lax.psum_scatter(grad_wout, axes, scatter_dimension=0, tiled=True).astype(f32)
    d_gated = lax.dot_general(
        cotangent, w_out_all, (((2,), (1,)), ((), ())), preferred_element_type=f32
    )
    grad_y, grad_z, grad_gate = gate_back(d_gated)
    dy_b = grad_y.astype(bf16).reshape(batch, block_len, head_count, head_width)
    dy_float = dy_b.astype(f32)
    state_grad = jnp.einsum("bthn,bthp->bhpn", scaled_b, dy_b, preferred_element_type=f32)
    adjoint = relay(block_decay, state_grad, -1)
    grad_skip = jnp.sum(dy_float * x_float, axis=(0, 1, 3))
    d_mixing = jnp.einsum("bthp,bshp->bhts", dy_b, x_values, preferred_element_type=f32)
    dx_within = jnp.einsum("bhts,bthp->bshp", mixing_b, dy_b, preferred_element_type=f32)
    d_affinity, d_cum_mix, d_step_mix = mixing_back(d_mixing)
    d_scaled = jnp.einsum("bthp,bhpn->bthn", dy_b, state_b, preferred_element_type=f32)
    d_read_state, d_cum_state = scale_back(d_scaled)
    d_decay = jnp.sum(adjoint * state_in, axis=(2, 3))
    adjoint_b = adjoint.astype(bf16)
    d_weighted = jnp.einsum("bhpn,bsn->bshp", adjoint_b, write_rows, preferred_element_type=f32)
    dwrite_state = jnp.einsum("bshp,bhpn->bsn", weighted_b, adjoint_b, preferred_element_type=f32)
    dx_state = d_weighted * weight_end[..., None]
    d_wend = jnp.sum(d_weighted * x_float, axis=3)
    d_cum_block, d_step_block = end_back((d_wend, d_decay))
    affinity_b = d_affinity.astype(bf16)
    d_read = (
        jnp.einsum("bts,bsn->btn", affinity_b, write_rows, preferred_element_type=f32)
        + d_read_state
    )
    d_write = (
        jnp.einsum("bts,btn->bsn", affinity_b, read_rows, preferred_element_type=f32)
        + dwrite_state
    )
    dx_total = dx_within + dx_state + d_skip[:, None] * dy_float
    d_act = jnp.concatenate(
        [dx_total.reshape(batch, block_len, inner_width), d_write, d_read], axis=2
    )
    d_ext, d_dtraw, d_convw, d_convb, d_dtbias, d_alog = mixer_back(
        (d_act, d_step_mix + d_step_block, d_cum_mix + d_cum_state + d_cum_block)
    )
    rim_grad = shifted(d_ext[:, :3], "seq", -1)
    d_xbc = d_ext[:, 3:] + jnp.pad(rim_grad, ((0, 0), (block_len - 3, 0), (0, 0)))
    d_proj = jnp.concatenate([grad_z, d_xbc, d_dtraw], axis=2).astype(bf16)
    d_normed = lax.dot_general(
        d_proj, w_in_all, (((2,), (1,)), ((), ())), preferred_element_type=f32
    )
    dx_norm, grad_gain = norm_back(d_normed)
    grad_rows = (cot_f + dx_norm).astype(bf16)
    grad_win = lax.dot_general(
        normed_b, d_proj, (((0, 1), (0, 1)), ((), ())), preferred_element_type=f32
    ).astype(bf16)

    heads = jnp.concatenate([d_dtbias, d_alog, grad_skip])
    pieces = jnp.concatenate(
        [
            grad_gain.reshape(all_devices, -1),
            d_convw.reshape(4, all_devices, -1).swapaxes(0, 1).reshape(all_devices, -1),
            d_convb.reshape(all_devices, -1),
            grad_gate.reshape(all_devices, -1),
            jnp.broadcast_to(heads, (all_devices, heads.size)),
        ],
        axis=1,
    )
    half = proj_width // 2
    grad_cols = -(-pieces.shape[1] // (2 * slab_rows))
    pieces = jnp.pad(pieces, ((0, 0), (0, 2 * grad_cols * slab_rows - pieces.shape[1])))
    halves = jnp.stack(
        [
            grad_win[:, :half].reshape(all_devices, slab_rows, half),
            grad_win[:, half:].reshape(all_devices, slab_rows, half),
        ],
        axis=1,
    )
    packed = jnp.concatenate(
        [halves, pieces.reshape(all_devices, 2, slab_rows, grad_cols).astype(bf16)], axis=3
    ).reshape(2 * model_width, half + grad_cols)
    summed = lax.psum_scatter(packed, axes, scatter_dimension=0, tiled=True).astype(f32)
    small_sum = summed[:, half:].reshape(-1)
    grad_win_own = jnp.concatenate([summed[:slab_rows, :half], summed[slab_rows:, :half]], axis=1)
    ends = bounds + [bounds[-1] + head_count * i for i in (1, 2, 3)]
    part = [small_sum[ends[i] : ends[i + 1]] for i in range(7)]
    return (
        result_rows,
        grad_rows,
        part[0],
        grad_win_own,
        part[1].reshape(4, -1),
        part[2],
        part[4],
        part[5],
        part[6],
        part[3],
        grad_wout,
    )


def solution(mesh):
    placed = (
        P("dp", "seq", None),
        P("dp", "seq", None),
        P("dp", None),
        P(("dp", "seq")),
        P(("dp", "seq"), None),
        P(None, ("dp", "seq")),
        P(("dp", "seq")),
        P(),
        P(),
        P(),
        P(("dp", "seq")),
        P(("dp", "seq"), None),
    )
    return jax.shard_map(
        per_device,
        mesh=mesh,
        in_specs=placed,
        out_specs=(
            P("dp", "seq", None),
            P("dp", "seq", None),
            P(("dp", "seq")),
            P(("dp", "seq"), None),
            P(None, ("dp", "seq")),
            P(("dp", "seq")),
            P(),
            P(),
            P(),
            P(("dp", "seq")),
            P(("dp", "seq"), None),
        ),
        check_vma=False,
    )
```

```python
from functools import partial

import jax
import jax.numpy as jnp
from jax import lax
from jax.sharding import PartitionSpec as P

EPSILON = 1e-05
CONTRACT_ROWS = (((0,), (0,)), ((), ()))
CONTRACT_COLS = (((1,), (1,)), ((), ()))


def hop(value, axis, source, target):
    return lax.ppermute(value, axis, [(source, target)])


def shifted(value, axis, steps):
    count = lax.axis_size(axis)
    initial, last = (max(0, -steps), min(count, count - steps))
    return lax.ppermute(value, axis, [(source, source + steps) for source in range(initial, last)])


def norm_input(tokens_f, gain_f):
    inv = lax.rsqrt(jnp.mean(tokens_f * tokens_f, axis=-1, keepdims=True) + EPSILON)
    return tokens_f * inv * gain_f


def mixer_inputs(xbc_ext, dt_raw, conv_w, conv_b, dt_bias, a_log, tap_mask):
    block_len = dt_raw.shape[1]
    pre = conv_b
    for offset in range(4):
        pre = (
            pre
            + conv_w[offset]
            * xbc_ext[:, offset : offset + block_len]
            * tap_mask[:, :, offset : offset + 1]
        )
    activated = jax.nn.silu(pre)
    step_size = jax.nn.softplus(dt_raw + dt_bias)
    cumulated = jnp.cumsum(-jnp.exp(a_log) * step_size, axis=1)
    return (activated, step_size, cumulated)


def mixing_weights(affinity, cumulated, step_size, same_doc):
    cum_heads = jnp.swapaxes(cumulated, 1, 2)
    exponent = jnp.where(
        same_doc[:, None], cum_heads[:, :, :, None] - cum_heads[:, :, None, :], -1e30
    )
    return affinity[:, None] * jnp.exp(exponent) * jnp.swapaxes(step_size, 1, 2)[:, :, None, :]


def end_weights(cumulated, step_size, end_same, carried_last):
    weight_end = jnp.exp(cumulated[:, -1:] - cumulated) * step_size * end_same[:, :, None]
    block_decay = jnp.exp(cumulated[:, -1]) * carried_last[:, None]
    return (weight_end, block_decay)


def read_scale(read_float, cumulated, carried):
    factor = jnp.exp(cumulated) * carried[:, :, None]
    return factor[:, :, :, None] * read_float[:, :, None, :]


def gate_norm(y_values, z_float, gain_f):
    gated_in = y_values * jax.nn.silu(z_float)
    return (
        gated_in
        * lax.rsqrt(jnp.mean(gated_in * gated_in, axis=-1, keepdims=True) + EPSILON)
        * gain_f
    )


def relay(decay, local, direction):
    count = lax.axis_size("seq")
    chains = []
    for index in range(local.shape[0]):
        incoming = jnp.zeros_like(local[index])
        for step in range(count - 1):
            source = step if direction > 0 else count - 1 - step
            outgoing = decay[index][:, None, None] * incoming + local[index]
            arrived = hop(outgoing.astype(jnp.bfloat16), "seq", source, source + direction)
            incoming = incoming + arrived.astype(jnp.float32)
        chains.append(incoming)
    return jnp.stack(chains)


def per_device(
    block_input,
    cotangent,
    segments,
    norm_gain,
    w_in,
    conv_weight,
    conv_bias,
    dt_bias,
    a_log,
    d_skip,
    gate_gain,
    w_out,
):
    batch, block_len, model_width = block_input.shape
    axes = ("dp", "seq")
    all_devices = lax.axis_size(axes)
    block_start = lax.axis_index("seq") * block_len
    inner_width = gate_gain.shape[0] * all_devices
    head_count = dt_bias.shape[0]
    head_width = inner_width // head_count
    xbc_width = conv_bias.shape[0] * all_devices
    state_width = (xbc_width - inner_width) // 2
    proj_width = w_in.shape[1]
    slab_rows = w_in.shape[0]
    f32 = jnp.float32
    bf16 = jnp.bfloat16

    small_sizes = (norm_gain.size, conv_weight.size, conv_bias.size, gate_gain.size)
    small_cols = -(-sum(small_sizes) // slab_rows)
    smalls = jnp.concatenate(
        [norm_gain, conv_weight.reshape(-1), conv_bias, gate_gain,
         jnp.zeros((small_cols * slab_rows - sum(small_sizes),), bf16)]
    ).reshape(slab_rows, small_cols)
    rest_width = proj_width - inner_width
    w_rest_full = lax.all_gather(
        jnp.concatenate([w_in[:, inner_width:], smalls], axis=1), axes, axis=0, tiled=True
    )
    w_rest_full, w_gate_own, w_out_own = lax.optimization_barrier(
        (w_rest_full, w_in[:, :inner_width], w_out)
    )
    w_gate_all = lax.all_gather(w_gate_own, axes, axis=0, tiled=True)
    w_out_all = lax.all_gather(w_out_own, axes, axis=0, tiled=True)
    w_rest_all = w_rest_full[:, :rest_width]
    small_all = w_rest_full[:, rest_width:].reshape(all_devices, slab_rows * small_cols)
    bounds = [0]
    for size in small_sizes:
        bounds.append(bounds[-1] + size)
    gain_all = small_all[:, bounds[0] : bounds[1]].reshape(-1).astype(f32)
    conv_w_all = (
        small_all[:, bounds[1] : bounds[2]]
        .reshape(all_devices, 4, -1)
        .swapaxes(0, 1)
        .reshape(4, xbc_width)
        .astype(f32)
    )
    conv_b_all = small_all[:, bounds[2] : bounds[3]].reshape(-1).astype(f32)
    gate_all = small_all[:, bounds[3] : bounds[4]].reshape(-1).astype(f32)

    tokens_f = block_input.astype(f32)
    normed, norm_back = jax.vjp(norm_input, tokens_f, gain_all)
    normed_b = normed.astype(bf16)
    projected = lax.dot_general(
        normed_b, w_rest_all, (((2,), (0,)), ((), ())), preferred_element_type=f32
    ).astype(bf16)
    z_rows = lax.dot_general(
        normed_b, w_gate_all, (((2,), (0,)), ((), ())), preferred_element_type=f32
    ).astype(bf16)
    xbc_rows = projected[:, :, :xbc_width]
    rim_rows = shifted(xbc_rows[:, block_len - 3 :], "seq", 1)
    padded = jnp.concatenate([jnp.full((batch, 3), -1, jnp.int32), segments], axis=1)
    seg_window = lax.dynamic_slice_in_dim(padded, block_start, block_len + 3, axis=1)
    seg_local = seg_window[:, 3:]
    tap_mask = jnp.stack(
        [seg_window[:, offset : offset + block_len] == seg_local for offset in range(4)], axis=2
    ).astype(f32)
    xbc_ext = jnp.concatenate([rim_rows, xbc_rows], axis=1).astype(f32)
    dt_raw = projected[:, :, xbc_width:].astype(f32)
    (activated, step_size, cumulated), mixer_back = jax.vjp(
        partial(mixer_inputs, tap_mask=tap_mask),
        xbc_ext,
        dt_raw,
        conv_w_all,
        conv_b_all,
        dt_bias,
        a_log,
    )
    act_b = activated.astype(bf16)
    x_values = act_b[:, :, :inner_width].reshape(batch, block_len, head_count, head_width)
    write_rows = act_b[:, :, inner_width : inner_width + state_width]
    read_rows = act_b[:, :, inner_width + state_width :]
    prior_segment = seg_window[:, 2:3]
    positions = lax.iota(jnp.int32, block_len)
    same_doc = (seg_local[:, :, None] == seg_local[:, None, :]) & (
        positions[None, :] <= positions[:, None]
    )
    carried = (seg_local == prior_segment).astype(f32)
    end_same = (seg_local == seg_local[:, -1:]).astype(f32)
    x_float = x_values.astype(f32)
    read_float = read_rows.astype(f32)
    (weight_end, block_decay), end_back = jax.vjp(
        partial(end_weights, end_same=end_same, carried_last=carried[:, -1]), cumulated, step_size
    )
    weighted_b = (x_float * weight_end[..., None]).astype(bf16)
    local_state = jnp.einsum("bshp,bsn->bhpn", weighted_b, write_rows, preferred_element_type=f32)
    state_in = relay(block_decay, local_state, 1)
    state_b = state_in.astype(bf16)
    affinity = jnp.einsum("btn,bsn->bts", read_rows, write_rows, preferred_element_type=f32)
    mixing, mixing_back = jax.vjp(
        partial(mixing_weights, same_doc=same_doc), affinity, cumulated, step_size
    )
    mixing_b = mixing.astype(bf16)
    within = jnp.einsum("bhts,bshp->bthp", mixing_b, x_values, preferred_element_type=f32)
    scaled, scale_back = jax.vjp(partial(read_scale, carried=carried), read_float, cumulated)
    scaled_b = scaled.astype(bf16)
    from_state = jnp.einsum("bthn,bhpn->bthp", scaled_b, state_b, preferred_element_type=f32)
    y_heads = within + from_state + d_skip[:, None] * x_float
    z_float = z_rows.astype(f32)
    gated, gate_back = jax.vjp(
        gate_norm, y_heads.reshape(batch, block_len, inner_width), z_float, gate_all
    )
    gated_b = gated.astype(bf16)
    mixed = lax.dot_general(
        gated_b, w_out_all, (((2,), (0,)), ((), ())), preferred_element_type=f32
    )
    result_rows = (tokens_f + mixed).astype(bf16)
    cot_f = cotangent.astype(f32)
    grad_wout = lax.dot_general(
        gated_b, cotangent, (((0, 1), (0, 1)), ((), ())), preferred_element_type=f32
    ).astype(bf16)
    d_gated = lax.dot_general(
        cotangent, w_out_all, (((2,), (1,)), ((), ())), preferred_element_type=f32
    )
    grad_y, grad_z, grad_gate = gate_back(d_gated)
    dz_b = grad_z.astype(bf16)

    def halved(value):
        half = value.shape[1] // 2
        return jnp.stack(
            [
                value[:, :half].reshape(all_devices, slab_rows, half),
                value[:, half:].reshape(all_devices, slab_rows, half),
            ],
            axis=1,
        )

    def unhalved(value):
        return jnp.concatenate([value[:slab_rows], value[slab_rows:]], axis=1)

    grad_wz = lax.dot_general(
        normed_b, dz_b, (((0, 1), (0, 1)), ((), ())), preferred_element_type=f32
    ).astype(bf16)
    grad_wz = halved(grad_wz).reshape(2 * model_width, inner_width // 2)
    dy_b, grad_wz, grad_wout = lax.optimization_barrier(
        (grad_y.astype(bf16), grad_wz, grad_wout)
    )
    grad_wout = lax.psum_scatter(grad_wout, axes, scatter_dimension=0, tiled=True).astype(f32)
    grad_wz = lax.psum_scatter(grad_wz, axes, scatter_dimension=0, tiled=True).astype(f32)
    skip_cols = jnp.sum(
        dy_b.astype(f32) * act_b[:, :, :inner_width].astype(f32), axis=(0, 1)
    )
    grad_skip = jnp.sum(skip_cols.reshape(head_count, head_width), axis=1)
    dy_b = dy_b.reshape(batch, block_len, head_count, head_width)
    dy_float = dy_b.astype(f32)
    state_grad = jnp.einsum("bthn,bthp->bhpn", scaled_b, dy_b, preferred_element_type=f32)
    adjoint = relay(block_decay, state_grad, -1)
    d_mixing = jnp.einsum("bthp,bshp->bhts", dy_b, x_values, preferred_element_type=f32)
    dx_within = jnp.einsum("bhts,bthp->bshp", mixing_b, dy_b, preferred_element_type=f32)
    d_affinity, d_cum_mix, d_step_mix = mixing_back(d_mixing)
    d_scaled = jnp.einsum("bthp,bhpn->bthn", dy_b, state_b, preferred_element_type=f32)
    d_read_state, d_cum_state = scale_back(d_scaled)
    d_decay = jnp.sum(adjoint * state_in, axis=(2, 3))
    adjoint_b = adjoint.astype(bf16)
    d_weighted = jnp.einsum("bhpn,bsn->bshp", adjoint_b, write_rows, preferred_element_type=f32)
    dwrite_state = jnp.einsum("bshp,bhpn->bsn", weighted_b, adjoint_b, preferred_element_type=f32)
    dx_state = d_weighted * weight_end[..., None]
    d_wend = jnp.sum(d_weighted * x_float, axis=3)
    d_cum_block, d_step_block = end_back((d_wend, d_decay))
    affinity_b = d_affinity.astype(bf16)
    d_read = (
        jnp.einsum("bts,bsn->btn", affinity_b, write_rows, preferred_element_type=f32)
        + d_read_state
    )
    d_write = (
        jnp.einsum("bts,btn->bsn", affinity_b, read_rows, preferred_element_type=f32)
        + dwrite_state
    )
    dx_total = dx_within + dx_state + d_skip[:, None] * dy_float
    d_act = jnp.concatenate(
        [dx_total.reshape(batch, block_len, inner_width), d_write, d_read], axis=2
    )
    d_ext, d_dtraw, d_convw, d_convb, d_dtbias, d_alog = mixer_back(
        (d_act, d_step_mix + d_step_block, d_cum_mix + d_cum_state + d_cum_block)
    )
    rim_grad = shifted(d_ext[:, :3], "seq", -1)
    d_xbc = d_ext[:, 3:] + jnp.pad(rim_grad, ((0, 0), (block_len - 3, 0), (0, 0)))
    d_rest = jnp.concatenate([d_xbc, d_dtraw], axis=2).astype(bf16)
    d_normed = lax.dot_general(
        dz_b, w_gate_all, (((2,), (1,)), ((), ())), preferred_element_type=f32
    ) + lax.dot_general(
        d_rest, w_rest_all, (((2,), (1,)), ((), ())), preferred_element_type=f32
    )
    dx_norm, grad_gain = norm_back(d_normed)
    grad_rows = (cot_f + dx_norm).astype(bf16)
    grad_rest = lax.dot_general(
        normed_b, d_rest, (((0, 1), (0, 1)), ((), ())), preferred_element_type=f32
    ).astype(bf16)

    heads = jnp.concatenate([d_dtbias, d_alog, grad_skip])
    pieces = jnp.concatenate(
        [
            grad_gain.reshape(all_devices, -1),
            d_convw.reshape(4, all_devices, -1).swapaxes(0, 1).reshape(all_devices, -1),
            d_convb.reshape(all_devices, -1),
            grad_gate.reshape(all_devices, -1),
            jnp.broadcast_to(heads, (all_devices, heads.size)),
        ],
        axis=1,
    )
    half = rest_width // 2
    grad_cols = -(-pieces.shape[1] // (2 * slab_rows))
    pieces = jnp.pad(pieces, ((0, 0), (0, 2 * grad_cols * slab_rows - pieces.shape[1])))
    packed = jnp.concatenate(
        [halved(grad_rest), pieces.reshape(all_devices, 2, slab_rows, grad_cols).astype(bf16)], axis=3
    ).reshape(2 * model_width, half + grad_cols)
    summed = lax.psum_scatter(packed, axes, scatter_dimension=0, tiled=True).astype(f32)
    small_sum = summed[:, half:].reshape(-1)
    grad_win_own = jnp.concatenate([unhalved(grad_wz), unhalved(summed[:, :half])], axis=1)
    ends = bounds + [bounds[-1] + head_count * i for i in (1, 2, 3)]
    part = [small_sum[ends[i] : ends[i + 1]] for i in range(7)]
    return (
        result_rows,
        grad_rows,
        part[0],
        grad_win_own,
        part[1].reshape(4, -1),
        part[2],
        part[4],
        part[5],
        part[6],
        part[3],
        grad_wout,
    )


def solution(mesh):
    placed = (
        P("dp", "seq", None),
        P("dp", "seq", None),
        P("dp", None),
        P(("dp", "seq")),
        P(("dp", "seq"), None),
        P(None, ("dp", "seq")),
        P(("dp", "seq")),
        P(),
        P(),
        P(),
        P(("dp", "seq")),
        P(("dp", "seq"), None),
    )
    return jax.shard_map(
        per_device,
        mesh=mesh,
        in_specs=placed,
        out_specs=(
            P("dp", "seq", None),
            P("dp", "seq", None),
            P(("dp", "seq")),
            P(("dp", "seq"), None),
            P(None, ("dp", "seq")),
            P(("dp", "seq")),
            P(),
            P(),
            P(),
            P(("dp", "seq")),
            P(("dp", "seq"), None),
        ),
        check_vma=False,
    )
```
